256 devices in a mesh: grp: 8 (over y, core), sub: 32 (over z, x).
Axes of the slice: x: 4, y: 4, z: 8, core: 2. Of those that a mesh axis runs over, the one named last changes fastest.
Arguments:
- iterate: bfloat16 [262144, 1024], P(('grp', 'sub')), may hold values from -6 to 6
- load: bfloat16 [262144, 1024], P(('grp', 'sub')), may hold values from -6 to 6
- schur: bfloat16 [262144, 1024], P(('grp', 'sub'))
- local_inverse: bfloat16 [262144, 1024], P(('grp', 'sub'))
- basis: bfloat16 [6144, 1024], P(('grp', 'sub')), may hold values from -0.1875 to 0.1875
- coarse_inverse: float32 [1024, 1024], P('grp')
- owner: int32 [256, 24], P(('grp', 'sub')), may hold values from 0 to 1023, as said below
- shared_index: int32 [256, 6, 224], P(('grp', 'sub')), may hold values from 0 to 1023, as said below
- shared_count: int32 [256, 6], P(('grp', 'sub')), may hold values from 179 to 224, as said below
Outputs:
- new_iterate: bfloat16 [262144, 1024], P(('grp', 'sub'))
- residual: bfloat16 [262144, 1024], P(('grp', 'sub'))
The draws below stay inside these ranges and needn't reach their ends.
Inputs may be any that keep to these rules, and one draw needn't show every extreme that they name: shared_count[i, j] equals shared_count[b, j xor 1] for i and its neighbour j named b; in every group some pair shares exactly 224 dofs. `shared_index`: the live slots of one subdomain toward one neighbour name distinct dofs, and every interface dof of a subdomain lies in some live slot of it. `owner`: A subdomain of group g names coarse dofs of the blocks g, g + 1, g - 1 or g + 4 (modulo 8) of 128 coarse dofs each.
All inputs are finite; a program needn't handle non-finite values.
Results may differ from the reference program's by a relative error of at most 0.012.
Values may be sent and summed in bfloat16 or wider, within the bound.
A program may use at most 192 MiB of HBM per device.

```python
import jax
import jax.numpy as jnp
from jax import lax

NI = 1024
NRHS = 1024
CAP = 224
NC = 24
CG = 128
SUBDOMAINS = 256
NCG = 1024
N_GRP = 8
N_SUB = 32


def dominant_draw(key, row_total, col_total):
    first_key, second_key = jax.random.split(key, 2)
    row_ids = lax.broadcasted_iota(jnp.int32, (row_total, col_total), 0) % col_total
    col_ids = lax.broadcasted_iota(jnp.int32, (row_total, col_total), 1)
    diagonal = 1.0 + jax.random.uniform(second_key, (row_total, 1), jnp.float32, 0.0, 1.0)
    noise = jax.random.normal(first_key, (row_total, col_total), jnp.float32)
    spread = 0.5 / jnp.sqrt(jnp.float32(col_total))
    return jnp.where(row_ids == col_ids, diagonal, 0.0) + spread * noise


def draw_schur(key, part):
    return dominant_draw(jax.random.fold_in(key, 3), SUBDOMAINS * NI, NI).astype(jnp.bfloat16)


def draw_local_inverse(key, part):
    return dominant_draw(jax.random.fold_in(key, 5), SUBDOMAINS * NI, NI).astype(jnp.bfloat16)


def draw_coarse_inverse(key, part):
    return dominant_draw(jax.random.fold_in(key, 7), NCG, NCG)


def draw_owner(key, part):
    first_key, second_key = jax.random.split(jax.random.fold_in(key, 9))
    group_ids = jnp.arange(SUBDOMAINS, dtype=jnp.int32)[:, None] // N_SUB
    pick = jax.random.randint(first_key, (SUBDOMAINS, NC), 0, 8)
    offset = jnp.where(pick == 6, 1, jnp.where(pick == 7, -1, 0))
    first_column = lax.broadcasted_iota(jnp.int32, (SUBDOMAINS, NC), 1) == 0
    offset = jnp.where(first_column, N_GRP // 2, offset)
    target = (group_ids + offset + N_GRP) % N_GRP
    return (target * CG + jax.random.randint(second_key, (SUBDOMAINS, NC), 0, CG)).astype(jnp.int32)


def pair_tables(key):
    first_key, second_key = jax.random.split(key)
    lowest = CAP * 4 // 5
    raw = jax.random.randint(first_key, (N_GRP, N_SUB, 3), 0, 1048576)
    pair_count = lowest + raw % (CAP - lowest + 1)
    first_pair = (lax.broadcasted_iota(jnp.int32, (N_GRP, N_SUB, 3), 1) == 0) & (lax.broadcasted_iota(jnp.int32, (N_GRP, N_SUB, 3), 2) == 0)
    pair_count = jnp.where(first_pair, CAP, pair_count).astype(jnp.int32)
    sides = []
    for step in range(3):
        forward = pair_count[:, :, step]
        sides.append(forward)
        sides.append(jnp.roll(forward, step + 1, axis=1))
    counts = jnp.stack(sides, axis=2).reshape(SUBDOMAINS, 6)
    sub_keys = jax.random.split(second_key, SUBDOMAINS)
    orders = jax.vmap(lambda one_key: jax.random.permutation(one_key, NI))(sub_keys).astype(jnp.int32)
    starts = jnp.cumsum(counts, axis=1) - counts
    slot_ids = jnp.arange(CAP, dtype=jnp.int32)
    places = (starts[:, :, None] + slot_ids[None, None, :]) % NI
    index = jnp.take_along_axis(orders, places.reshape(SUBDOMAINS, 6 * CAP), axis=1)
    return (counts.astype(jnp.int32), index.reshape(SUBDOMAINS, 6, CAP).astype(jnp.int32))


def draw_shared_count(key, part):
    return pair_tables(jax.random.fold_in(key, 11))[0]


def draw_shared_index(key, part):
    return pair_tables(jax.random.fold_in(key, 11))[1]


def level_of(stream_key, dims, cuts, least, high):
    factor_of = 1.0
    for axis_at, parts in cuts:
        steps = jax.random.uniform(jax.random.fold_in(jax.random.fold_in(stream_key, 6), axis_at), (parts,), jnp.float32, least / len(cuts), high / len(cuts))
        factor_of = factor_of * jnp.repeat(jnp.exp(steps), dims[axis_at] // parts).reshape((-1,) + (1,) * (len(dims) - 1 - axis_at))
    return factor_of


def normal_values(own_key, dims, deviation, most, pieces=(), kind=jnp.bfloat16):
    loudness = level_of(own_key, dims, pieces, -0.22, 0.18) if pieces else 1.0
    values = jax.random.normal(own_key, dims, jnp.float32) * deviation * loudness
    return jnp.minimum(jnp.maximum(values, -most), most).astype(kind)


def setup_inputs(seed: int = 0) -> dict:
    streams_of = jax.random.split(jax.random.key(seed), 10)
    iterate = normal_values(streams_of[0], (SUBDOMAINS * NI, NRHS), 1.0, 6.0, ((0, 256),))
    load = normal_values(streams_of[1], (SUBDOMAINS * NI, NRHS), 1.0, 6.0, ((0, 256),))
    schur = draw_schur(jax.random.fold_in(streams_of[9], 71), 0)
    local_inverse = draw_local_inverse(jax.random.fold_in(streams_of[9], 71), 0)
    basis = normal_values(streams_of[4], (SUBDOMAINS * NC, NI), NI ** -0.5, 0.1875, ((0, 256),))
    coarse_inverse = draw_coarse_inverse(jax.random.fold_in(streams_of[9], 71), 0)
    owner = draw_owner(jax.random.fold_in(streams_of[9], 71), 0)
    shared_index = draw_shared_index(jax.random.fold_in(streams_of[9], 71), 0)
    shared_count = draw_shared_count(jax.random.fold_in(streams_of[9], 71), 0)
    return dict(iterate=iterate, load=load, schur=schur, local_inverse=local_inverse, basis=basis, coarse_inverse=coarse_inverse, owner=owner, shared_index=shared_index, shared_count=shared_count)


def live_slots(shared_count):
    slot_ids = lax.broadcasted_iota(jnp.int32, (shared_count.shape[0], shared_count.shape[1], CAP), 2)
    return slot_ids < shared_count[:, :, None]


def assemble(values, shared_index, live, finish):
    distance = jnp.array([1, -1, 2, -2, 3, -3], jnp.int32)
    mirror = jnp.array([1, 0, 3, 2, 5, 4], jnp.int32)

    def one_subdomain(sub_id):
        group_base = (sub_id // N_SUB) * N_SUB
        own_slot = sub_id % N_SUB
        own_index = shared_index[sub_id]
        own_live = live[sub_id]
        peer_ids = group_base + (own_slot + distance + N_SUB) % N_SUB
        peer_index = shared_index[peer_ids, mirror]
        peer_rows = values[peer_ids[:, None], peer_index].astype(jnp.float32)
        incoming = jnp.where(own_live[:, :, None], peer_rows, jnp.zeros_like(peer_rows))
        total = values[sub_id].astype(jnp.float32)
        total = total.at[own_index.reshape(-1)].add(incoming.reshape(-1, NRHS))
        return finish(sub_id, total)
    return lax.map(one_subdomain, jnp.arange(SUBDOMAINS, dtype=jnp.int32))


def reference(iterate, load, schur, local_inverse, basis, coarse_inverse, owner, shared_index, shared_count):
    high = lax.Precision.HIGHEST
    sub_range = jnp.arange(SUBDOMAINS, dtype=jnp.int32)
    iterate_blocks = iterate.reshape(SUBDOMAINS, NI, NRHS)
    load_blocks = load.reshape(SUBDOMAINS, NI, NRHS)
    schur_blocks = schur.reshape(SUBDOMAINS, NI, NI)
    inverse_blocks = local_inverse.reshape(SUBDOMAINS, NI, NI)
    basis_blocks = basis.reshape(SUBDOMAINS, NC, NI)
    live = live_slots(shared_count)
    sub_ids = jnp.broadcast_to(sub_range[:, None, None], shared_index.shape)
    multiplicity = jnp.ones((SUBDOMAINS, NI), jnp.float32).at[sub_ids, shared_index].add(live.astype(jnp.float32))
    weight = 1.0 / multiplicity

    def local_step(sub_id):
        product = jnp.dot(schur_blocks[sub_id], iterate_blocks[sub_id], preferred_element_type=jnp.float32)
        return (load_blocks[sub_id].astype(jnp.float32) - product).astype(jnp.bfloat16)

    local_residual = lax.map(local_step, sub_range)

    def finish_residual(sub_id, total):
        return total.astype(jnp.bfloat16), (weight[sub_id][:, None] * total).astype(jnp.bfloat16)

    residual, scaled = assemble(local_residual, shared_index, live, finish_residual)

    def coarse_step(sub_id):
        return jnp.dot(basis_blocks[sub_id], scaled[sub_id], preferred_element_type=jnp.float32)

    coarse_terms = lax.map(coarse_step, sub_range)
    coarse_residual = jnp.zeros((NCG, NRHS), jnp.float32).at[owner.reshape(-1)].add(coarse_terms.reshape(-1, NRHS))
    coarse_values = jnp.dot(coarse_inverse, coarse_residual, precision=high, preferred_element_type=jnp.float32)

    def correction_step(sub_id):
        own_values = coarse_values[owner[sub_id]]
        coarse_part = jnp.dot(basis_blocks[sub_id].astype(jnp.float32).T, own_values, precision=high, preferred_element_type=jnp.float32)
        local_part = jnp.dot(inverse_blocks[sub_id], scaled[sub_id], preferred_element_type=jnp.float32)
        return (weight[sub_id][:, None] * (local_part + coarse_part)).astype(jnp.bfloat16)

    correction = lax.map(correction_step, sub_range)

    def finish_update(sub_id, total):
        return (iterate_blocks[sub_id].astype(jnp.float32) + total).astype(jnp.bfloat16)

    new_iterate = assemble(correction, shared_index, live, finish_update)
    return new_iterate.reshape(SUBDOMAINS * NI, NRHS), residual.reshape(SUBDOMAINS * NI, NRHS)
```

```python
import functools

import jax
import jax.numpy as jnp
from jax import lax
from jax.experimental import pallas as pl
from jax.experimental.pallas import tpu as pltpu
from jax.sharding import PartitionSpec as P

MESH = pl.DeviceIdType.MESH
OFFSETS = (1, -1, 2, -2, 3, -3)
REL_BLOCKS = (0, 1, 4, 7)
NI = 1024
CAP = 224
SLOT = 256
SIDES = 6
NC = 24
ROWS = SIDES * SLOT
CHUNKS = 4
WIDE = NI // CHUNKS
N_SUB = 32
N_Z = 8
N_X = 4
N_GRP = 8
F32 = jnp.float32
BF16 = jnp.bfloat16


def dot(a, b):
    return jnp.dot(a, b, preferred_element_type=F32)


def dot_nt(a, b):
    return lax.dot_general(a, b, (((1,), (1,)), ((), ())), preferred_element_type=F32)


def dot_tn(a, b):
    return lax.dot_general(a, b, (((0,), (0,)), ((), ())), preferred_element_type=F32)


def split(x):
    high = x.astype(BF16)
    return high, (x - high.astype(F32)).astype(BF16)


def kernel(
    u_hbm, f_hbm, s_hbm, k_hbm, p_ref, cinv_hbm, own_ref, idx_ref,
    new_hbm, res_hbm,
    u, f, s, k, cinv, pick, pick_t, wcol, wp,
    rb, cb, out1, in1, out2, in2, stage,
    terms, gathered, etr, rel_sum, rel_in, all_sum, rel_val, own_val, near_val,
    y_out, y_in, bt,
    load_sem, a1_send, a1_recv, a2_send, a2_recv, y_send, y_recv,
    s1_send, s1_recv, s2_send, s2_recv, s3_send, s3_recv, s4_send, s4_recv,
    s5_send, s5_recv, s6_send, s6_recv, store_sem,
):
    g = lax.axis_index("grp")
    a = lax.axis_index("sub")
    z = a // N_X
    x = lax.rem(a, N_X)

    def near(j):
        return {"sub": lax.rem(a + OFFSETS[j] + N_SUB, N_SUB)}

    def along_z(d):
        return {"sub": lax.rem(z + d, N_Z) * N_X + x}

    def along_x(d):
        return {"sub": z * N_X + lax.rem(x + d, N_X)}

    def along_g(d):
        return {"grp": lax.rem(g + d, N_GRP)}

    def remote(src, dst, send, recv, where):
        return pltpu.make_async_remote_copy(
            src_ref=src, dst_ref=dst, send_sem=send, recv_sem=recv,
            device_id=where, device_id_type=MESH,
        )

    loads = [
        pltpu.make_async_copy(src, dst, load_sem.at[n])
        for n, (src, dst) in enumerate(
            ((s_hbm, s), (u_hbm, u), (f_hbm, f), (k_hbm, k), (cinv_hbm, cinv))
        )
    ]
    for load in loads:
        load.start()

    barrier = pltpu.get_barrier_semaphore()
    partners = [near(j) for j in range(SIDES)]
    partners += [along_z(d) for d in range(1, N_Z)]
    partners += [along_x(d) for d in range(1, N_X)]
    partners += [along_g(d) for d in range(1, N_GRP)]
    for who in partners:
        pl.semaphore_signal(barrier, inc=1, device_id=who, device_id_type=MESH)

    lane = lax.broadcasted_iota(jnp.int32, (SLOT, 128), 1).astype(F32)
    for j in range(SIDES):
        row = idx_ref[j : j + 1, :]
        column = jnp.transpose(jnp.broadcast_to(row, (128, SLOT)))
        for q in range(NI // 128):
            pick[SLOT * j : SLOT * (j + 1), 128 * q : 128 * (q + 1)] = jnp.where(
                column == lane + float(128 * q), 1.0, 0.0
            ).astype(BF16)

    pl.semaphore_wait(barrier, len(partners))

    def assembly_copy(out, into, send, recv, c, j):
        return remote(
            out.at[c, pl.ds(SLOT * j, CAP), :],
            into.at[c, pl.ds(SLOT * (j ^ 1), CAP), :],
            send.at[c, j],
            recv.at[c, j ^ 1],
            near(j),
        )

    def assembly_wait(out, into, send, recv, c, j):
        remote(
            out.at[c, pl.ds(SLOT * j, CAP), :],
            into.at[c, pl.ds(SLOT * j, CAP), :],
            send.at[c, j],
            recv.at[c, j],
            near(j),
        ).wait_recv()

    for n in range(3):
        loads[n].wait()

    def first(c, carry):
        columns = pl.ds(pl.multiple_of(c * WIDE, WIDE), WIDE)
        rest = (f[:, columns].astype(F32) - dot(s[...], u[:, columns])).astype(BF16)
        rb[c] = rest
        out1[c] = dot(pick[...], rest).astype(BF16)
        for j in range(SIDES):
            assembly_copy(out1, in1, a1_send, a1_recv, c, j).start()
        return carry

    lax.fori_loop(0, CHUNKS, first, 0)

    up = lax.broadcasted_iota(jnp.int32, (NI, SLOT), 0).astype(F32)
    for j in range(SIDES):
        pick_t[:, SLOT * j : SLOT * (j + 1)] = jnp.where(
            idx_ref[j : j + 1, :] == up, 1.0, 0.0
        ).astype(BF16)
    wcol[...] = 1.0 / (1.0 + dot(pick_t[...], jnp.ones((ROWS, 128), BF16)))
    wrow = 1.0 / (1.0 + dot(jnp.ones((8, ROWS), BF16), pick[...]))
    weighted = p_ref[...].astype(F32) * wrow[0:1, :]
    zero8 = jnp.zeros((8, NI), F32)
    wp[...] = jnp.concatenate([weighted, zero8], axis=0).astype(BF16)
    for j in range(SIDES):
        y_out[j] = dot_nt(wp[...], pick[SLOT * j : SLOT * (j + 1), :]).astype(BF16)
        remote(y_out.at[j], y_in.at[j ^ 1], y_send.at[j], y_recv.at[j ^ 1], near(j)).start()
    for c in range(CHUNKS):
        for j in range(SIDES):
            rows = slice(SLOT * j + CAP, SLOT * (j + 1))
            in1[c, rows, :] = jnp.zeros((SLOT - CAP, WIDE), BF16)
            in2[c, rows, :] = jnp.zeros((SLOT - CAP, WIDE), BF16)
    for n in range(N_Z):
        terms[n, NC:32, :] = own_ref[...]
        near_val[n, 7] = jnp.zeros((32, 128), BF16)
    loads[3].wait()
    loads[4].wait()

    def weights():
        return jnp.concatenate([wcol[...]] * (WIDE // 128), axis=1)

    def send_second(c):
        for j in range(SIDES):
            assembly_copy(out2, in2, a2_send, a2_recv, c, j).start()

    def second(c, carry):
        for j in range(SIDES):
            assembly_wait(out1, in1, a1_send, a1_recv, c, j)
        total = rb[c].astype(F32) + dot(pick_t[...], in1[c])
        columns = pl.ds(pl.multiple_of(c * WIDE, WIDE), WIDE)
        stage[0, c] = total.astype(BF16)
        pltpu.make_async_copy(stage.at[0, c], res_hbm.at[:, columns], store_sem.at[0, c]).start()
        scaled = (weights() * total).astype(BF16)
        part = dot(p_ref[...], scaled)
        for q in range(WIDE // 128):
            terms[c * (WIDE // 128) + q, 0:NC, :] = part[:, 128 * q : 128 * (q + 1)]
        local = (weights() * dot(k[...], scaled)).astype(BF16)
        cb[c] = local
        out2[c] = dot(pick[...], local).astype(BF16)

        @pl.when(c == 0)
        def _():
            send_second(c)

        return carry

    lax.fori_loop(0, CHUNKS, second, 0)

    def z_copy(d):
        there = lax.rem(z + d, N_Z)
        return remote(
            terms.at[there], gathered.at[x, z], s1_send.at[d - 1], s1_recv.at[d - 1], along_z(d)
        )

    for d in range(1, N_Z):
        z_copy(d).start()
    gathered[x, z] = terms[z]
    for d in range(1, N_Z):
        here = lax.rem(z + N_Z - d, N_Z)
        remote(
            terms.at[z], gathered.at[x, here], s1_send.at[d - 1], s1_recv.at[d - 1], along_z(d)
        ).wait_recv()

    def x_copy(d):
        return remote(
            gathered.at[x], gathered.at[x], s2_send.at[d - 1], s2_recv.at[d - 1], along_x(d)
        )

    for d in range(1, N_X):
        x_copy(d).start()

    def issue(c, carry):
        send_second(c)
        return carry

    lax.fori_loop(1, CHUNKS, issue, 0)

    for j in range(SIDES):
        remote(y_out.at[j], y_in.at[j], y_send.at[j], y_recv.at[j], near(j)).wait_recv()
    blocks = []
    for t in range(7):
        o = t - 3
        if o == 0:
            blocks.append(wp[...].astype(F32))
        else:
            j = OFFSETS.index(o)
            blocks.append(dot(y_in[j], pick[SLOT * j : SLOT * (j + 1), :]))
    blocks.append(jnp.zeros((32, NI), F32))
    bt[...] = jnp.transpose(jnp.concatenate(blocks, axis=0)).astype(BF16)

    for d in range(1, N_X):
        here = lax.rem(x + N_X - d, N_X)
        remote(
            gathered.at[x], gathered.at[here], s2_send.at[d - 1], s2_recv.at[d - 1], along_x(d)
        ).wait_recv()

    column512 = lax.broadcasted_iota(jnp.int32, (32, 512), 1)
    block = column512 // 128
    names = (
        column512 - block * 128
        + jnp.where(block == 1, 128, jnp.where(block == 2, 512, jnp.where(block == 3, 896, 0)))
    ).astype(F32)
    base = (g * 128).astype(F32)
    for xx in range(N_X):
        plane = jnp.concatenate([gathered[xx, zz] for zz in range(N_Z)], axis=0)
        turned = jnp.transpose(plane)
        for zz in range(N_Z):
            who = turned[0:32, 32 * zz + NC : 32 * zz + NC + 1]
            rel = who - base
            rel = jnp.where(rel < 0.0, rel + 1024.0, rel)
            rel = jnp.where(who < 0.0, -1.0, rel)
            etr[256 * xx + 32 * zz : 256 * xx + 32 * (zz + 1), :] = jnp.where(
                rel == names, 1.0, 0.0
            ).astype(BF16)
    flat = jnp.concatenate(
        [gathered[xx, zz] for xx in range(N_X) for zz in range(N_Z)], axis=0
    )
    high, low = split(flat)
    sums = dot_tn(etr[...], high) + dot_tn(etr[...], low)
    for n in range(4):
        rel_sum[n] = sums[128 * n : 128 * (n + 1), :]
    for n in range(1, 4):
        remote(
            rel_sum.at[n], rel_in.at[n - 1], s3_send.at[n - 1], s3_recv.at[n - 1],
            along_g(REL_BLOCKS[n]),
        ).start()
    for n in range(1, 4):
        remote(
            rel_sum.at[n], rel_in.at[n - 1], s3_send.at[n - 1], s3_recv.at[n - 1],
            along_g(REL_BLOCKS[n]),
        ).wait_recv()
    all_sum[g] = rel_sum[0] + rel_in[0] + rel_in[1] + rel_in[2]
    for d in range(1, N_GRP):
        remote(
            all_sum.at[g], all_sum.at[g], s4_send.at[d - 1], s4_recv.at[d - 1], along_g(d)
        ).start()
    for d in range(1, N_GRP):
        here = lax.rem(g + N_GRP - d, N_GRP)
        remote(
            all_sum.at[g], all_sum.at[here], s4_send.at[d - 1], s4_recv.at[d - 1], along_g(d)
        ).wait_recv()
    high, low = split(all_sum[...].reshape(NI, 128))
    chigh, clow = split(cinv[...])
    rel_val[0] = dot(chigh, high) + (dot(chigh, low) + dot(clow, high))
    for n, d in ((1, 7), (2, 4), (3, 1)):
        remote(
            rel_val.at[0], rel_val.at[n], s5_send.at[n - 1], s5_recv.at[n - 1], along_g(d)
        ).start()
    for n, d in ((1, 7), (2, 4), (3, 1)):
        remote(
            rel_val.at[0], rel_val.at[n], s5_send.at[n - 1], s5_recv.at[n - 1], along_g(d)
        ).wait_recv()
    high, low = split(rel_val[...].reshape(512, 128))
    values = (dot(etr[...], high) + dot(etr[...], low)).astype(BF16)
    for xx in range(N_X):
        for zz in range(N_Z):
            piece = values[256 * xx + 32 * zz : 256 * xx + 32 * (zz + 1), :]
            place = zz * N_X + xx + 3
            own_val[place] = piece
            if place >= N_SUB:
                own_val[place - N_SUB] = piece
            if place < 6:
                own_val[place + N_SUB] = piece
    for d in range(1, N_Z):
        there = lax.rem(z + d, N_Z)
        remote(
            own_val.at[pl.ds(there * N_X + x, 7)], near_val.at[z, pl.ds(0, 7)],
            s6_send.at[d - 1], s6_recv.at[d - 1], along_z(d),
        ).start()
    near_val[z, pl.ds(0, 7)] = own_val[pl.ds(a, 7)]
    for d in range(1, N_Z):
        here = lax.rem(z + N_Z - d, N_Z)
        remote(
            own_val.at[pl.ds(a, 7)], near_val.at[here, pl.ds(0, 7)],
            s6_send.at[d - 1], s6_recv.at[d - 1], along_z(d),
        ).wait_recv()

    def third(c, carry):
        columns = pl.ds(pl.multiple_of(c * WIDE, WIDE), WIDE)
        coarse = jnp.concatenate(
            [near_val[c * (WIDE // 128) + q].reshape(256, 128) for q in range(WIDE // 128)], axis=1
        )
        part = u[:, columns].astype(F32) + (cb[c].astype(F32) + dot(bt[...], coarse))
        for j in range(SIDES):
            assembly_wait(out2, in2, a2_send, a2_recv, c, j)
        stage[1, c] = (part + dot(pick_t[...], in2[c])).astype(BF16)
        pltpu.make_async_copy(stage.at[1, c], new_hbm.at[:, columns], store_sem.at[1, c]).start()
        return carry

    lax.fori_loop(0, CHUNKS, third, 0)

    def finish(c, carry):
        columns = pl.ds(pl.multiple_of(c * WIDE, WIDE), WIDE)
        for j in range(SIDES):
            assembly_copy(out1, in1, a1_send, a1_recv, c, j).wait_send()
            assembly_copy(out2, in2, a2_send, a2_recv, c, j).wait_send()
        pltpu.make_async_copy(stage.at[0, c], res_hbm.at[:, columns], store_sem.at[0, c]).wait()
        pltpu.make_async_copy(stage.at[1, c], new_hbm.at[:, columns], store_sem.at[1, c]).wait()
        return carry

    lax.fori_loop(0, CHUNKS, finish, 0)
    for j in range(SIDES):
        remote(y_out.at[j], y_in.at[j ^ 1], y_send.at[j], y_recv.at[j ^ 1], near(j)).wait_send()
    for d in range(1, N_Z):
        z_copy(d).wait_send()
        there = lax.rem(z + d, N_Z)
        remote(
            own_val.at[pl.ds(there * N_X + x, 7)], near_val.at[z, pl.ds(0, 7)],
            s6_send.at[d - 1], s6_recv.at[d - 1], along_z(d),
        ).wait_send()
        remote(
            all_sum.at[g], all_sum.at[g], s4_send.at[d - 1], s4_recv.at[d - 1], along_g(d)
        ).wait_send()
    for d in range(1, N_X):
        x_copy(d).wait_send()
    for n in range(1, 4):
        remote(
            rel_sum.at[n], rel_in.at[n - 1], s3_send.at[n - 1], s3_recv.at[n - 1],
            along_g(REL_BLOCKS[n]),
        ).wait_send()
        remote(
            rel_val.at[0], rel_val.at[n], s5_send.at[n - 1], s5_recv.at[n - 1], along_g(1)
        ).wait_send()


def on_device(
    iterate, load, schur, local_inverse, basis, coarse_inverse, owner, shared_index, shared_count
):
    live = lax.broadcasted_iota(jnp.int32, (SIDES, CAP), 1) < shared_count[0][:, None]
    index = jnp.where(live, shared_index[0], -1).astype(F32)
    index = jnp.pad(index, ((0, 8 - SIDES), (0, SLOT - CAP)), constant_values=-1.0)
    names = jnp.pad(owner.astype(F32), ((0, 0), (0, 128 - NC)), constant_values=-1.0)
    names = jnp.broadcast_to(names, (8, 128))
    anywhere = pl.BlockSpec(memory_space=pl.ANY)
    vmem = pl.BlockSpec(memory_space=pltpu.VMEM)
    square = jax.ShapeDtypeStruct((NI, NI), BF16)
    dma = pltpu.SemaphoreType.DMA
    new, residual = pl.pallas_call(
        kernel,
        out_shape=(square, square),
        in_specs=[anywhere, anywhere, anywhere, anywhere, vmem, anywhere, vmem, vmem],
        out_specs=(anywhere, anywhere),
        scratch_shapes=[
            pltpu.VMEM((NI, NI), BF16),
            pltpu.VMEM((NI, NI), BF16),
            pltpu.VMEM((NI, NI), BF16),
            pltpu.VMEM((NI, NI), BF16),
            pltpu.VMEM((128, NI), F32),
            pltpu.VMEM((ROWS, NI), BF16),
            pltpu.VMEM((NI, ROWS), BF16),
            pltpu.VMEM((NI, 128), F32),
            pltpu.VMEM((32, NI), BF16),
            pltpu.VMEM((CHUNKS, NI, WIDE), BF16),
            pltpu.VMEM((CHUNKS, NI, WIDE), BF16),
            pltpu.VMEM((CHUNKS, ROWS, WIDE), BF16),
            pltpu.VMEM((CHUNKS, ROWS, WIDE), BF16),
            pltpu.VMEM((CHUNKS, ROWS, WIDE), BF16),
            pltpu.VMEM((CHUNKS, ROWS, WIDE), BF16),
            pltpu.VMEM((2, CHUNKS, NI, WIDE), BF16),
            pltpu.VMEM((N_Z, 32, 128), F32),
            pltpu.VMEM((N_X, N_Z, 32, 128), F32),
            pltpu.VMEM((NI, 512), BF16),
            pltpu.VMEM((4, 128, 128), F32),
            pltpu.VMEM((3, 128, 128), F32),
            pltpu.VMEM((N_GRP, 128, 128), F32),
            pltpu.VMEM((4, 128, 128), F32),
            pltpu.VMEM((N_SUB + 6, 32, 128), BF16),
            pltpu.VMEM((N_Z, 8, 32, 128), BF16),
            pltpu.VMEM((SIDES, 32, SLOT), BF16),
            pltpu.VMEM((SIDES, 32, SLOT), BF16),
            pltpu.VMEM((NI, 256), BF16),
            dma((5,)),
            dma((CHUNKS, SIDES)),
            dma((CHUNKS, SIDES)),
            dma((CHUNKS, SIDES)),
            dma((CHUNKS, SIDES)),
            dma((SIDES,)),
            dma((SIDES,)),
            dma((7,)), dma((7,)),
            dma((3,)), dma((3,)),
            dma((3,)), dma((3,)),
            dma((7,)), dma((7,)),
            dma((3,)), dma((3,)),
            dma((7,)), dma((7,)),
            dma((2, CHUNKS)),
        ],
        compiler_params=pltpu.CompilerParams(
            collective_id=0, has_side_effects=True, vmem_limit_bytes=60 * 1024 * 1024
        ),
        name="bddc_step",
    )(iterate, load, schur, local_inverse, basis, coarse_inverse, names, index)
    return new, residual


def solution(mesh):
    rows = P(("grp", "sub"), None)
    placed = (rows, rows, rows, rows, rows, P("grp", None), rows, P(("grp", "sub"), None, None), rows)
    return jax.shard_map(
        on_device, mesh=mesh, in_specs=placed, out_specs=(rows, rows), check_vma=False
    )
```

```python
import jax
import jax.numpy as jnp
from jax import lax
from jax.experimental import pallas as pl
from jax.experimental.pallas import tpu as pltpu
from jax.sharding import PartitionSpec as P

MESH = pl.DeviceIdType.MESH
OFFSETS = (1, -1, 2, -2, 3, -3)
NI = 1024
CAP = 224
SLOT = 256
SIDES = 6
NC = 24
ROWS = SIDES * SLOT
CHUNKS = 4
WIDE = NI // CHUNKS
N_SUB = 32
N_Z = 8
N_X = 4
N_GRP = 8
NCG = 1024
LIMIT = 49 * 1024 * 1024
EARLY = 2
PER = WIDE // 128
TALL = 176
F32 = jnp.float32
BF16 = jnp.bfloat16


def dot(a, b):
    return jnp.dot(a, b, preferred_element_type=F32)


def dot_nt(a, b):
    return lax.dot_general(a, b, (((1,), (1,)), ((), ())), preferred_element_type=F32)


def dot_tn(a, b):
    return lax.dot_general(a, b, (((0,), (0,)), ((), ())), preferred_element_type=F32)


def split(x):
    high = x.astype(BF16)
    return high, (x - high.astype(F32)).astype(BF16)


def kernel(
    u_hbm, f_hbm, s_hbm, k_hbm, p_ref, cinv_hbm, own_ref, idx_ref, cnt_ref,
    new_ref, res_ref,
    u, f, s, k, cinv, slots, pick, pick_t, wcol, wp,
    rb, cb, out1, in1, out2, in2,
    owners, btr, bt, y_out, y_in, terms, terms_in, etr, t_out, t_in, pieces,
    v_out, v_in, rel_val, own_val, near_val, early,
    load_sem, a1_send, a1_recv, a2_send, a2_recv, y_send, y_recv,
    s1_send, s1_recv, s2_send, s2_recv, s3_send, s3_recv, s4_send, s4_recv,
    s5_send, s5_recv, s6_send, s6_recv,
):
    g = lax.axis_index("grp")
    a = lax.axis_index("sub")
    z = a // N_X
    x = lax.rem(a, N_X)

    def near(j):
        return {"sub": lax.rem(a + OFFSETS[j] + N_SUB, N_SUB)}

    def along_z(d):
        return {"sub": lax.rem(z + d, N_Z) * N_X + x}

    def along_x(d):
        return {"sub": z * N_X + lax.rem(x + d, N_X)}

    def along_g(d):
        return {"grp": lax.rem(g + d, N_GRP)}

    def remote(src, dst, send, recv, where):
        return pltpu.make_async_remote_copy(
            src_ref=src, dst_ref=dst, send_sem=send, recv_sem=recv,
            device_id=where, device_id_type=MESH,
        )

    loads = [pltpu.make_async_copy(s_hbm, s, load_sem.at[0])]
    for c in range(CHUNKS):
        cols = pl.ds(c * WIDE, WIDE)
        for n, (src, dst) in enumerate(((u_hbm, u), (f_hbm, f))):
            loads.append(
                pltpu.make_async_copy(src.at[:, cols], dst.at[c], load_sem.at[1 + 2 * c + n])
            )
    late_loads = [
        pltpu.make_async_copy(k_hbm, k, load_sem.at[1 + 2 * CHUNKS]),
        pltpu.make_async_copy(cinv_hbm, cinv, load_sem.at[2 + 2 * CHUNKS]),
    ]
    for load in loads + late_loads:
        load.start()

    barrier = pltpu.get_barrier_semaphore()
    partners = [near(j) for j in range(SIDES)]
    partners += [along_z(d) for d in range(1, N_Z)]
    partners += [along_x(d) for d in range(1, N_X)]
    partners += [along_g(d) for d in range(1, N_GRP)]
    for who in partners:
        pl.semaphore_signal(barrier, inc=1, device_id=who, device_id_type=MESH)

    slots[...] = jnp.full((8, SLOT), -1.0, F32)
    slot_ids = lax.broadcasted_iota(jnp.int32, (1, CAP), 1)
    for j in range(SIDES):
        slots[j : j + 1, 0:CAP] = jnp.where(
            slot_ids < cnt_ref[0, j], idx_ref[0, j : j + 1, :].astype(F32), -1.0
        )
    lane = lax.broadcasted_iota(jnp.int32, (SLOT, 128), 1).astype(F32)
    counts = [jnp.zeros((8, 128), F32)] * (NI // 128)
    for j in range(SIDES):
        column = jnp.transpose(jnp.broadcast_to(slots[j : j + 1, :], (128, SLOT)))
        for q in range(NI // 128):
            hot = jnp.where(column == lane + float(128 * q), 1.0, 0.0)
            pick[SLOT * j : SLOT * (j + 1), 128 * q : 128 * (q + 1)] = hot.astype(BF16)
            counts[q] += jnp.sum(hot.reshape(SLOT // 8, 8, 128), axis=0)
    wrow = 1.0 / (1.0 + jnp.sum(jnp.concatenate(counts, axis=1), axis=0, keepdims=True))

    def first(c):
        if c == 0:
            loads[0].wait()
        loads[1 + 2 * c].wait()
        loads[2 + 2 * c].wait()
        rest = (f[c].astype(F32) - dot(s[...], u[c])).astype(BF16)
        rb[c] = rest
        out1[c] = dot(pick[...], rest).astype(BF16)

    def assembly_copy(out, into, send, recv, c, j):
        return remote(
            out.at[c, pl.ds(SLOT * j, CAP), :],
            into.at[c, pl.ds(SLOT * (j ^ 1), CAP), :],
            send.at[c, j],
            recv.at[c, j ^ 1],
            near(j),
        )

    def assembly_wait(out, into, send, recv, c, j):
        remote(
            out.at[c, pl.ds(SLOT * j, CAP), :],
            into.at[c, pl.ds(SLOT * j, CAP), :],
            send.at[c, j],
            recv.at[c, j],
            near(j),
        ).wait_recv()

    def send_first(c):
        for j in range(SIDES):
            assembly_copy(out1, in1, a1_send, a1_recv, c, j).start()

    def send_second(c, sides=range(SIDES)):
        for j in sides:
            assembly_copy(out2, in2, a2_send, a2_recv, c, j).start()

    weighted = p_ref[...].astype(F32) * wrow
    wp[...] = jnp.concatenate([weighted, jnp.zeros((8, NI), F32)], axis=0).astype(BF16)
    owners[...] = jnp.zeros((16, 128), F32)
    owners[8:9, 0:NC] = (own_ref[...] >> 5).astype(F32)
    owners[9:10, 0:NC] = (own_ref[...] & 31).astype(F32)
    low_names = pltpu.roll(jnp.broadcast_to(owners[9:10, :], (8, 128)), 64, 1)
    mine = jnp.broadcast_to(owners[8:9, :], (8, 128)) + low_names
    for j in range(SIDES):
        rows = dot_nt(wp[...], pick[SLOT * j : SLOT * (j + 1), :])
        tail = jnp.concatenate([mine, jnp.zeros((8, SLOT - 128), F32)], axis=1)
        y_out[j] = jnp.concatenate([rows[0:NC], tail], axis=0).astype(BF16)
    first(0)
    pl.semaphore_wait(barrier, len(partners))
    for j in range(SIDES):
        remote(y_out.at[j], y_in.at[j ^ 1], y_send.at[j], y_recv.at[j ^ 1], near(j)).start()
    send_first(0)

    for c in range(1, CHUNKS):
        first(c)
        if c < 2:
            send_first(c)

    for j in range(SIDES):
        remote(y_out.at[j], y_in.at[j], y_send.at[j], y_recv.at[j], near(j)).wait_recv()
    blocks = []
    for t in range(7):
        if t == 3:
            blocks.append(wp[0:NC, :].astype(F32))
            owners[t : t + 1, :] = mine[0:1, :]
        else:
            j = OFFSETS.index(t - 3)
            blocks.append(dot(y_in[j], pick[SLOT * j : SLOT * (j + 1), :])[0:NC])
            owners[t : t + 1, :] = y_in[j, NC:32, 0:128].astype(F32)[0:1, :]
    blocks.append(jnp.zeros((256 - 7 * NC, NI), F32))
    every = jnp.concatenate(blocks, axis=0)
    btr[...] = every[0:TALL].astype(BF16)
    for c in range(CHUNKS):
        part = dot(btr[...], rb[c])
        for q in range(PER):
            terms[c * PER + q] = jnp.concatenate(
                [part[0 : 7 * NC, 128 * q : 128 * (q + 1)], owners[0:8, :]], axis=0
            ).astype(BF16)

    def z_copy(d):
        there = lax.rem(z + d, N_Z)
        return remote(
            terms.at[there], terms_in.at[z], s1_send.at[d - 1], s1_recv.at[d - 1], along_z(d)
        )

    for d in range(1, N_Z):
        z_copy(d).start()
    send_first(2)
    terms_in[z] = terms[z]

    up = lax.broadcasted_iota(jnp.int32, (NI, SLOT), 0).astype(F32)
    for j in range(SIDES):
        pick_t[:, SLOT * j : SLOT * (j + 1)] = jnp.where(
            slots[j : j + 1, :] == up, 1.0, 0.0
        ).astype(BF16)
    wcol[...] = 1.0 / (1.0 + dot(pick_t[...], jnp.ones((ROWS, 128), BF16)))
    for c in range(CHUNKS):
        for j in range(SIDES):
            rows = slice(SLOT * j + CAP, SLOT * (j + 1))
            in1[c, rows, :] = jnp.zeros((SLOT - CAP, WIDE), BF16)
            in2[c, rows, :] = jnp.zeros((SLOT - CAP, WIDE), BF16)
    for n in range(N_Z):
        near_val[n, TALL:256, :] = jnp.zeros((256 - TALL, 128), BF16)
    for load in late_loads:
        load.wait()

    bt[...] = jnp.transpose(every).astype(BF16)
    for d in range(1, N_Z):
        here = lax.rem(z + N_Z - d, N_Z)
        remote(
            terms.at[z], terms_in.at[here], s1_send.at[d - 1], s1_recv.at[d - 1], along_z(d)
        ).wait_recv()

    weights = jnp.concatenate([wcol[...]] * (WIDE // 128), axis=1)

    def second(c):
        for j in range(SIDES):
            assembly_wait(out1, in1, a1_send, a1_recv, c, j)
        total = rb[c].astype(F32) + dot(pick_t[...], in1[c])
        res_ref[:, c * WIDE : (c + 1) * WIDE] = total.astype(BF16)
        scaled = (weights * total).astype(BF16)
        local = (weights * dot(k[...], scaled)).astype(BF16)
        cb[c] = local
        out2[c] = dot(pick[...], local).astype(BF16)

    column512 = lax.broadcasted_iota(jnp.int32, (NC, 512), 1)
    block = column512 // 128
    start = block + 2 * (block // 2) + 2 * (block // 3)
    names = (column512 + 128 * (start - block)).astype(F32)
    base = (g * 128).astype(F32)
    turned = jnp.transpose(
        jnp.concatenate([terms_in[n, TALL - 16 : TALL, :].astype(F32)[8:16] for n in range(N_Z)], axis=0)
    )
    who = turned[0:NC, :] * 32.0 + turned[64 : 64 + NC, :]
    rel = who - base
    rel = jnp.where(rel < 0.0, rel + float(NCG), rel)
    for n in range(N_Z):
        hot = [
            jnp.where(rel[:, 8 * n + t : 8 * n + t + 1] == names, 1.0, 0.0) for t in range(7)
        ]
        hot.append(jnp.zeros((8, 512), F32))
        etr[TALL * n : TALL * (n + 1), :] = jnp.concatenate(hot, axis=0).astype(BF16)
    sums = dot_tn(etr[...], terms_in[...].reshape(N_Z * TALL, 128)).reshape(4, 128, 128)
    t_out[...] = sums.astype(BF16)

    def x_copy(d):
        there = lax.rem(x + d, N_X)
        return remote(
            t_out.at[there], t_in.at[d - 1], s2_send.at[d - 1], s2_recv.at[d - 1], along_x(d)
        )

    for d in range(1, N_X):
        x_copy(d).start()
    second(0)
    send_first(3)
    for d in range(1, N_X):
        x_copy(d).wait_recv()
    own_block = t_out[x].astype(F32)
    for d in range(1, N_X):
        own_block += t_in[d - 1].astype(F32)
    named = lax.rem(g + x + 2 * (x // 2) + 2 * (x // 3), N_GRP)
    pieces[named] = own_block.astype(BF16)

    def g_copy(d):
        return remote(
            pieces.at[named], pieces.at[named], s3_send.at[d - 1], s3_recv.at[d - 1], along_g(d)
        )

    for d in range(1, N_GRP):
        g_copy(d).start()
    send_second(0)
    second(1)
    for d in range(1, N_GRP):
        here = lax.rem(named + N_GRP - d, N_GRP)
        remote(
            pieces.at[named], pieces.at[here], s3_send.at[d - 1], s3_recv.at[d - 1], along_g(d)
        ).wait_recv()
    chigh, clow = split(cinv[...])
    flat = pieces[...].reshape(NI, 128)
    partial = dot(chigh, flat) + dot(clow, flat)
    v_out[0] = partial.astype(BF16)

    def v_copy(d):
        return remote(
            v_out.at[0], v_in.at[d - 1], s4_send.at[d - 1], s4_recv.at[d - 1], along_x(d)
        )

    for d in range(1, N_X):
        v_copy(d).start()
    send_second(1, range(3))
    second(2)
    send_second(1, range(3, SIDES))
    for d in range(1, N_X):
        v_copy(d).wait_recv()
    solved = v_out[0].astype(F32)
    for d in range(1, N_X):
        solved += v_in[d - 1].astype(F32)
    rel_val[0] = solved.astype(BF16)

    def r_copy(n):
        return remote(
            rel_val.at[0], rel_val.at[n], s5_send.at[n - 1], s5_recv.at[n - 1],
            along_g((7, 4, 1)[n - 1]),
        )

    for n in range(1, 4):
        r_copy(n).start()
    send_second(2)
    second(3)
    for n in range(1, 4):
        r_copy(n).wait_recv()
    own_val[...] = dot(etr[...], rel_val[...].reshape(512, 128)).astype(BF16).reshape(N_Z, TALL, 128)

    def o_copy(d):
        there = lax.rem(z + d, N_Z)
        return remote(
            own_val.at[there], near_val.at[z, pl.ds(0, TALL)],
            s6_send.at[d - 1], s6_recv.at[d - 1], along_z(d),
        )

    for d in range(1, N_Z):
        o_copy(d).start()
    send_second(3)
    near_val[z, pl.ds(0, TALL)] = own_val[z]

    def second_sum(c):
        for j in range(SIDES):
            assembly_wait(out2, in2, a2_send, a2_recv, c, j)
        return u[c].astype(F32) + (cb[c].astype(F32) + dot(pick_t[...], in2[c]))

    for c in range(EARLY):
        early[c] = second_sum(c)
    for d in range(1, N_Z):
        here = lax.rem(z + N_Z - d, N_Z)
        remote(
            own_val.at[z], near_val.at[here, pl.ds(0, TALL)],
            s6_send.at[d - 1], s6_recv.at[d - 1], along_z(d),
        ).wait_recv()

    def third(c):
        coarse = dot(bt[...], jnp.concatenate([near_val[c * PER + q] for q in range(PER)], axis=1))
        if c < EARLY:
            total = early[c] + coarse
        else:
            total = u[c].astype(F32) + (cb[c].astype(F32) + coarse)
            for j in range(SIDES):
                assembly_wait(out2, in2, a2_send, a2_recv, c, j)
            total += dot(pick_t[...], in2[c])
        new_ref[:, c * WIDE : (c + 1) * WIDE] = total.astype(BF16)

    for c in range(CHUNKS):
        third(c)

    for c in range(CHUNKS):
        for j in range(SIDES):
            assembly_copy(out1, in1, a1_send, a1_recv, c, j).wait_send()
            assembly_copy(out2, in2, a2_send, a2_recv, c, j).wait_send()
    for j in range(SIDES):
        remote(y_out.at[j], y_in.at[j ^ 1], y_send.at[j], y_recv.at[j ^ 1], near(j)).wait_send()
    for d in range(1, N_Z):
        z_copy(d).wait_send()
        o_copy(d).wait_send()
        g_copy(d).wait_send()
    for d in range(1, N_X):
        x_copy(d).wait_send()
        v_copy(d).wait_send()
    for n in range(1, 4):
        r_copy(n).wait_send()


def on_device(
    iterate, load, schur, local_inverse, basis, coarse_inverse, owner, shared_index, shared_count
):
    anywhere = pl.BlockSpec(memory_space=pltpu.HBM)
    vmem = pl.BlockSpec(memory_space=pltpu.VMEM)
    smem = pl.BlockSpec(memory_space=pltpu.SMEM)
    square = jax.ShapeDtypeStruct((NI, NI), BF16)
    dma = pltpu.SemaphoreType.DMA

    def bf16(*shape):
        return pltpu.VMEM(shape, BF16)

    def f32(*shape):
        return pltpu.VMEM(shape, F32)

    chunk = (CHUNKS, NI, WIDE)
    side = (CHUNKS, ROWS, WIDE)
    return pl.pallas_call(
        kernel,
        out_shape=(square, square),
        in_specs=[anywhere, anywhere, anywhere, anywhere, vmem, anywhere, vmem, vmem, smem],
        out_specs=(vmem, vmem),
        scratch_shapes=[
            bf16(*chunk), bf16(*chunk), bf16(NI, NI), bf16(NI, NI), f32(128, NI),
            f32(8, SLOT), bf16(ROWS, NI), bf16(NI, ROWS), f32(NI, 128), bf16(32, NI),
            bf16(*chunk), bf16(*chunk), bf16(*side), bf16(*side), bf16(*side), bf16(*side),
            f32(16, 128), bf16(TALL, NI), bf16(NI, 256),
            bf16(SIDES, 32, SLOT), bf16(SIDES, 32, SLOT),
            bf16(N_Z, TALL, 128), bf16(N_Z, TALL, 128), bf16(N_Z * TALL, 512),
            bf16(4, 128, 128), bf16(3, 128, 128), bf16(N_GRP, 128, 128),
            bf16(1, 128, 128), bf16(3, 128, 128), bf16(4, 128, 128),
            bf16(N_Z, TALL, 128), bf16(N_Z, 256, 128), f32(EARLY, NI, WIDE),
            dma((3 + 2 * CHUNKS,)),
            dma((CHUNKS, SIDES)), dma((CHUNKS, SIDES)), dma((CHUNKS, SIDES)), dma((CHUNKS, SIDES)),
            dma((SIDES,)), dma((SIDES,)),
            dma((7,)), dma((7,)), dma((3,)), dma((3,)), dma((7,)), dma((7,)),
            dma((3,)), dma((3,)), dma((3,)), dma((3,)), dma((7,)), dma((7,)),
        ],
        compiler_params=pltpu.CompilerParams(
            collective_id=0, has_side_effects=True, vmem_limit_bytes=LIMIT
        ),
        name="bddc_step",
    )(
        iterate, load, schur, local_inverse, basis, coarse_inverse, owner, shared_index,
        shared_count,
    )


def solution(mesh):
    rows = P(("grp", "sub"), None)
    placed = (rows, rows, rows, rows, rows, P("grp", None), rows, P(("grp", "sub"), None, None), rows)
    return jax.shard_map(
        on_device, mesh=mesh, in_specs=placed, out_specs=(rows, rows), check_vma=False
    )
```

```python
import jax
import jax.numpy as jnp
from jax import lax
from jax.experimental import pallas as pl
from jax.experimental.pallas import tpu as pltpu
from jax.sharding import PartitionSpec as P

MESH = pl.DeviceIdType.MESH
OFFSETS = (1, -1, 2, -2, 3, -3)
NI = 1024
CAP = 224
SLOT = 256
SIDES = 6
NC = 24
ROWS = SIDES * SLOT
CHUNKS = 4
WIDE = NI // CHUNKS
N_SUB = 32
N_Z = 8
N_X = 4
N_GRP = 8
REL_BLOCKS = (0, 1, 4, 7)
NCG = 1024
LIMIT = 58 * 1024 * 1024
EARLY = 2
PER = WIDE // 128
TALL = 176
F32 = jnp.float32
BF16 = jnp.bfloat16


def dot(a, b):
    return jnp.dot(a, b, preferred_element_type=F32)


def dot_nt(a, b):
    return lax.dot_general(a, b, (((1,), (1,)), ((), ())), preferred_element_type=F32)


def dot_tn(a, b):
    return lax.dot_general(a, b, (((0,), (0,)), ((), ())), preferred_element_type=F32)


def split(x):
    high = x.astype(BF16)
    return high, (x - high.astype(F32)).astype(BF16)


def kernel(
    u_hbm, f_hbm, s_hbm, k_hbm, p_ref, cinv_hbm, own_ref, idx_ref, cnt_ref,
    new_ref, res_ref,
    u, f, s, k, cinv, slots, pick, pick_t, wcol, wp,
    rb, cb, out1, in1, out2, in2,
    owners, btr, bt, y_out, y_in, terms, terms_in, etr, pieces,
    v_out, v_in, rel_val, own_val, near_val, early,
    load_sem, a1_send, a1_recv, a2_send, a2_recv, y_send, y_recv,
    s1_send, s1_recv, s3_send, s3_recv, s4_send, s4_recv,
    s5_send, s5_recv, s6_send, s6_recv,
):
    g = lax.axis_index("grp")
    a = lax.axis_index("sub")
    z = a // N_X
    x = lax.rem(a, N_X)

    def near(j):
        return {"sub": lax.rem(a + OFFSETS[j] + N_SUB, N_SUB)}

    def along_z(d):
        return {"sub": lax.rem(z + d, N_Z) * N_X + x}

    def along_x(d):
        return {"sub": z * N_X + lax.rem(x + d, N_X)}

    def along_g(d):
        return {"grp": lax.rem(g + d, N_GRP)}

    def remote(src, dst, send, recv, where):
        return pltpu.make_async_remote_copy(
            src_ref=src, dst_ref=dst, send_sem=send, recv_sem=recv,
            device_id=where, device_id_type=MESH,
        )

    loads = [pltpu.make_async_copy(s_hbm, s, load_sem.at[0])]
    for c in range(CHUNKS):
        cols = pl.ds(c * WIDE, WIDE)
        for n, (src, dst) in enumerate(((u_hbm, u), (f_hbm, f))):
            loads.append(
                pltpu.make_async_copy(src.at[:, cols], dst.at[c], load_sem.at[1 + 2 * c + n])
            )
    late_loads = [
        pltpu.make_async_copy(k_hbm, k, load_sem.at[1 + 2 * CHUNKS]),
        pltpu.make_async_copy(cinv_hbm, cinv, load_sem.at[2 + 2 * CHUNKS]),
    ]
    for load in loads + late_loads:
        load.start()

    barrier = pltpu.get_barrier_semaphore()
    partners = [near(j) for j in range(SIDES)]
    partners += [along_z(d) for d in range(1, N_Z)]
    partners += [along_x(d) for d in range(1, N_X)]
    partners += [along_g(d) for d in range(1, N_GRP)]
    for who in partners:
        pl.semaphore_signal(barrier, inc=1, device_id=who, device_id_type=MESH)

    slots[...] = jnp.full((8, SLOT), -1.0, F32)
    slot_ids = lax.broadcasted_iota(jnp.int32, (1, CAP), 1)
    for j in range(SIDES):
        slots[j : j + 1, 0:CAP] = jnp.where(
            slot_ids < cnt_ref[0, j], idx_ref[j].astype(F32), -1.0
        )
    lane = lax.broadcasted_iota(jnp.int32, (SLOT, 128), 1).astype(F32)
    counts = [jnp.zeros((8, 128), F32)] * (NI // 128)
    for j in range(SIDES):
        column = jnp.transpose(jnp.broadcast_to(slots[j : j + 1, :], (128, SLOT)))
        for q in range(NI // 128):
            hot = jnp.where(column == lane + float(128 * q), 1.0, 0.0)
            pick[SLOT * j : SLOT * (j + 1), 128 * q : 128 * (q + 1)] = hot.astype(BF16)
            counts[q] += jnp.sum(hot.reshape(SLOT // 8, 8, 128), axis=0)
    wrow = 1.0 / (1.0 + jnp.sum(jnp.concatenate(counts, axis=1), axis=0, keepdims=True))

    def first(c):
        if c == 0:
            loads[0].wait()
        loads[1 + 2 * c].wait()
        loads[2 + 2 * c].wait()
        rest = (f[c].astype(F32) - dot(s[...], u[c])).astype(BF16)
        rb[c] = rest
        if c > 0:
            out1[c] = dot(pick[...], rest).astype(BF16)

    def assembly_copy(out, into, send, recv, c, j):
        return remote(
            out.at[c, pl.ds(SLOT * j, CAP), :],
            into.at[c, pl.ds(SLOT * (j ^ 1), CAP), :],
            send.at[c, j],
            recv.at[c, j ^ 1],
            near(j),
        )

    def assembly_wait(out, into, send, recv, c, j):
        remote(
            out.at[c, pl.ds(SLOT * j, CAP), :],
            into.at[c, pl.ds(SLOT * j, CAP), :],
            send.at[c, j],
            recv.at[c, j],
            near(j),
        ).wait_recv()

    def send_first(c, sides=range(SIDES)):
        for j in sides:
            assembly_copy(out1, in1, a1_send, a1_recv, c, j).start()

    def send_second(c, sides=range(SIDES)):
        for j in sides:
            assembly_copy(out2, in2, a2_send, a2_recv, c, j).start()

    weighted = p_ref[...].astype(F32) * wrow
    wp[...] = jnp.concatenate([weighted, jnp.zeros((8, NI), F32)], axis=0).astype(BF16)
    owners[...] = jnp.zeros((16, 128), F32)
    owners[8:9, 0:NC] = (own_ref[...] >> 5).astype(F32)
    owners[9:10, 0:NC] = (own_ref[...] & 31).astype(F32)
    low_names = pltpu.roll(jnp.broadcast_to(owners[9:10, :], (8, 128)), 64, 1)
    mine = jnp.broadcast_to(owners[8:9, :], (8, 128)) + low_names
    for j in range(SIDES):
        rows = dot_nt(wp[...], pick[SLOT * j : SLOT * (j + 1), :])
        tail = jnp.concatenate([mine, jnp.zeros((8, SLOT - 128), F32)], axis=1)
        y_out[j] = jnp.concatenate([rows[0:NC], tail], axis=0).astype(BF16)
    first(0)
    pl.semaphore_wait(barrier, len(partners))
    for j in range(SIDES):
        remote(y_out.at[j], y_in.at[j ^ 1], y_send.at[j], y_recv.at[j ^ 1], near(j)).start()
    for j in range(SIDES):
        rows = slice(SLOT * j, SLOT * (j + 1))
        out1[0, rows, :] = dot(pick[rows, :], rb[0]).astype(BF16)
        send_first(0, (j,))


    for c in range(1, CHUNKS):
        first(c)
        if c < 2:
            send_first(c)

    for j in range(SIDES):
        remote(y_out.at[j], y_in.at[j], y_send.at[j], y_recv.at[j], near(j)).wait_recv()
    blocks = []
    for t in range(7):
        if t == 3:
            blocks.append(wp[0:NC, :].astype(F32))
            owners[t : t + 1, :] = mine[0:1, :]
        else:
            j = OFFSETS.index(t - 3)
            blocks.append(dot(y_in[j], pick[SLOT * j : SLOT * (j + 1), :])[0:NC])
            owners[t : t + 1, :] = y_in[j, NC:32, 0:128].astype(F32)[0:1, :]
    blocks.append(jnp.zeros((256 - 7 * NC, NI), F32))
    every = jnp.concatenate(blocks, axis=0)
    btr[...] = every[0:TALL].astype(BF16)
    for c in range(CHUNKS):
        part = dot(btr[...], rb[c])
        for q in range(PER):
            terms[c * PER + q] = jnp.concatenate(
                [part[0 : 7 * NC, 128 * q : 128 * (q + 1)], owners[0:8, :]], axis=0
            ).astype(BF16)

    def z_copy(d):
        there = lax.rem(z + d, N_Z)
        return remote(
            terms.at[there], terms_in.at[z], s1_send.at[d - 1], s1_recv.at[d - 1], along_z(d)
        )

    for d in range(1, N_Z):
        z_copy(d).start()
    send_first(2)
    terms_in[z] = terms[z]

    up = lax.broadcasted_iota(jnp.int32, (NI, SLOT), 0).astype(F32)
    for j in range(SIDES):
        pick_t[:, SLOT * j : SLOT * (j + 1)] = jnp.where(
            slots[j : j + 1, :] == up, 1.0, 0.0
        ).astype(BF16)
    wcol[...] = 1.0 / (1.0 + dot(pick_t[...], jnp.ones((ROWS, 128), BF16)))
    for c in range(CHUNKS):
        for j in range(SIDES):
            rows = slice(SLOT * j + CAP, SLOT * (j + 1))
            in1[c, rows, :] = jnp.zeros((SLOT - CAP, WIDE), BF16)
            in2[c, rows, :] = jnp.zeros((SLOT - CAP, WIDE), BF16)
    for n in range(N_Z):
        near_val[n, TALL:256, :] = jnp.zeros((256 - TALL, 128), BF16)
    for load in late_loads:
        load.wait()

    bt[...] = jnp.transpose(every).astype(BF16)
    for d in range(1, N_Z):
        here = lax.rem(z + N_Z - d, N_Z)
        remote(
            terms.at[z], terms_in.at[here], s1_send.at[d - 1], s1_recv.at[d - 1], along_z(d)
        ).wait_recv()

    weights = jnp.concatenate([wcol[...]] * (WIDE // 128), axis=1)

    def second(c):
        for j in range(SIDES):
            assembly_wait(out1, in1, a1_send, a1_recv, c, j)
        total = rb[c].astype(F32) + dot(pick_t[...], in1[c])
        res_ref[:, c * WIDE : (c + 1) * WIDE] = total.astype(BF16)
        scaled = (weights * total).astype(BF16)
        local = (weights * dot(k[...], scaled)).astype(BF16)
        cb[c] = local
        out2[c] = dot(pick[...], local).astype(BF16)

    column512 = lax.broadcasted_iota(jnp.int32, (NC, 512), 1)
    block = column512 // 128
    start = block + 2 * (block // 2) + 2 * (block // 3)
    names = (column512 + 128 * (start - block)).astype(F32)
    base = (g * 128).astype(F32)
    turned = jnp.transpose(
        jnp.concatenate([terms_in[n, TALL - 16 : TALL, :].astype(F32)[8:16] for n in range(N_Z)], axis=0)
    )
    who = turned[0:NC, :] * 32.0 + turned[64 : 64 + NC, :]
    rel = who - base
    rel = jnp.where(rel < 0.0, rel + float(NCG), rel)
    for n in range(N_Z):
        hot = [
            jnp.where(rel[:, 8 * n + t : 8 * n + t + 1] == names, 1.0, 0.0) for t in range(7)
        ]
        hot.append(jnp.zeros((8, 512), F32))
        etr[TALL * n : TALL * (n + 1), :] = jnp.concatenate(hot, axis=0).astype(BF16)
    sums = dot_tn(etr[...], terms_in[...].reshape(N_Z * TALL, 128))
    pieces[g] = sums.astype(BF16).reshape(4, 128, 128)

    def g_copy(d):
        return remote(
            pieces.at[g], pieces.at[g], s3_send.at[d - 1], s3_recv.at[d - 1], along_g(d)
        )

    for d in range(1, N_GRP):
        g_copy(d).start()
    send_first(3)
    second(0)
    send_second(0, range(3))
    second(1)
    send_second(0, range(3, SIDES))
    for d in range(1, N_GRP):
        here = lax.rem(g + N_GRP - d, N_GRP)
        remote(
            pieces.at[g], pieces.at[here], s3_send.at[d - 1], s3_recv.at[d - 1], along_g(d)
        ).wait_recv()
    whole = [
        sum(pieces[(n - r) % N_GRP, q].astype(F32) for q, r in enumerate(REL_BLOCKS))
        for n in range(N_GRP)
    ]
    high, low = split(jnp.concatenate(whole, axis=0))
    chigh, clow = split(cinv[...])
    partial = dot(chigh, high) + (dot(clow, high) + dot(chigh, low))
    v_out[0] = partial.astype(BF16)

    def v_copy(d):
        return remote(
            v_out.at[0], v_in.at[d - 1], s4_send.at[d - 1], s4_recv.at[d - 1], along_x(d)
        )

    for d in range(1, N_X):
        v_copy(d).start()
    second(2)
    send_second(1, range(3))
    second(3)
    send_second(1, range(3, SIDES))
    send_second(2, range(3))
    for d in range(1, N_X):
        v_copy(d).wait_recv()
    solved = v_out[0].astype(F32)
    for d in range(1, N_X):
        solved += v_in[d - 1].astype(F32)
    rel_val[0] = solved.astype(BF16)

    def r_copy(n):
        return remote(
            rel_val.at[0], rel_val.at[n], s5_send.at[n - 1], s5_recv.at[n - 1],
            along_g((7, 4, 1)[n - 1]),
        )

    for n in range(1, 4):
        r_copy(n).start()
    send_second(2, range(3, SIDES))
    for n in range(1, 4):
        r_copy(n).wait_recv()
    own_val[...] = dot(etr[...], rel_val[...].reshape(512, 128)).astype(BF16).reshape(N_Z, TALL, 128)

    def o_copy(d):
        there = lax.rem(z + d, N_Z)
        return remote(
            own_val.at[there], near_val.at[z, pl.ds(0, TALL)],
            s6_send.at[d - 1], s6_recv.at[d - 1], along_z(d),
        )

    for d in range(1, N_Z):
        o_copy(d).start()
    send_second(3)
    near_val[z, pl.ds(0, TALL)] = own_val[z]

    def second_sum(c):
        for j in range(SIDES):
            assembly_wait(out2, in2, a2_send, a2_recv, c, j)
        return u[c].astype(F32) + (cb[c].astype(F32) + dot(pick_t[...], in2[c]))

    for c in range(EARLY):
        early[c] = second_sum(c)
    for d in range(1, N_Z):
        here = lax.rem(z + N_Z - d, N_Z)
        remote(
            own_val.at[z], near_val.at[here, pl.ds(0, TALL)],
            s6_send.at[d - 1], s6_recv.at[d - 1], along_z(d),
        ).wait_recv()

    def third(c):
        coarse = dot(bt[...], jnp.concatenate([near_val[c * PER + q] for q in range(PER)], axis=1))
        if c < EARLY:
            total = early[c] + coarse
        else:
            total = u[c].astype(F32) + (cb[c].astype(F32) + coarse)
            step = 2 if c == CHUNKS - 1 else SIDES
            for low in range(0, SIDES, step):
                for j in range(low, low + step):
                    assembly_wait(out2, in2, a2_send, a2_recv, c, j)
                rows = slice(SLOT * low, SLOT * (low + step))
                total += dot(pick_t[:, rows], in2[c, rows, :])
        new_ref[:, c * WIDE : (c + 1) * WIDE] = total.astype(BF16)

    for c in range(CHUNKS):
        third(c)

    for c in range(CHUNKS):
        for j in range(SIDES):
            assembly_copy(out1, in1, a1_send, a1_recv, c, j).wait_send()
            assembly_copy(out2, in2, a2_send, a2_recv, c, j).wait_send()
    for j in range(SIDES):
        remote(y_out.at[j], y_in.at[j ^ 1], y_send.at[j], y_recv.at[j ^ 1], near(j)).wait_send()
    for d in range(1, N_Z):
        z_copy(d).wait_send()
        o_copy(d).wait_send()
        g_copy(d).wait_send()
    for d in range(1, N_X):
        v_copy(d).wait_send()
    for n in range(1, 4):
        r_copy(n).wait_send()


def on_device(
    iterate, load, schur, local_inverse, basis, coarse_inverse, owner, shared_index, shared_count
):
    anywhere = pl.BlockSpec(memory_space=pltpu.HBM)
    vmem = pl.BlockSpec(memory_space=pltpu.VMEM)
    smem = pl.BlockSpec(memory_space=pltpu.SMEM)
    dma = pltpu.SemaphoreType.DMA

    def bf16(*shape):
        return pltpu.VMEM(shape, BF16)

    def f32(*shape):
        return pltpu.VMEM(shape, F32)

    chunk = (CHUNKS, NI, WIDE)
    side = (CHUNKS, ROWS, WIDE)
    new, residual = pl.pallas_call(
        kernel,
        out_shape=(bf16(NI, NI), bf16(NI, NI)),
        in_specs=[anywhere, anywhere, anywhere, anywhere, vmem, anywhere, vmem, vmem, smem],
        out_specs=(vmem, vmem),
        scratch_shapes=[
            bf16(*chunk), bf16(*chunk), bf16(NI, NI), bf16(NI, NI), f32(128, NI),
            f32(8, SLOT), bf16(ROWS, NI), bf16(NI, ROWS), f32(NI, 128), bf16(32, NI),
            bf16(*chunk), bf16(*chunk), bf16(*side), bf16(*side), bf16(*side), bf16(*side),
            f32(16, 128), bf16(TALL, NI), bf16(NI, 256),
            bf16(SIDES, 32, SLOT), bf16(SIDES, 32, SLOT),
            bf16(N_Z, TALL, 128), bf16(N_Z, TALL, 128), bf16(N_Z * TALL, 512),
            bf16(N_GRP, 4, 128, 128),
            bf16(1, 128, 128), bf16(3, 128, 128), bf16(4, 128, 128),
            bf16(N_Z, TALL, 128), bf16(N_Z, 256, 128), f32(EARLY, NI, WIDE),
            dma((3 + 2 * CHUNKS,)),
            dma((CHUNKS, SIDES)), dma((CHUNKS, SIDES)), dma((CHUNKS, SIDES)), dma((CHUNKS, SIDES)),
            dma((SIDES,)), dma((SIDES,)),
            dma((7,)), dma((7,)), dma((7,)), dma((7,)),
            dma((3,)), dma((3,)), dma((3,)), dma((3,)), dma((7,)), dma((7,)),
        ],
        compiler_params=pltpu.CompilerParams(
            collective_id=0, has_side_effects=True, vmem_limit_bytes=LIMIT
        ),
        name="bddc_step",
    )(
        iterate, load, schur, local_inverse, basis, coarse_inverse, owner,
        jnp.transpose(shared_index, (1, 0, 2)), shared_count,
    )
    return new, residual


def solution(mesh):
    rows = P(("grp", "sub"), None)
    placed = (rows, rows, rows, rows, rows, P("grp", None), rows, P(("grp", "sub"), None, None), rows)
    return jax.shard_map(
        on_device, mesh=mesh, in_specs=placed, out_specs=(rows, rows), check_vma=False
    )
```

```python
import jax
import jax.numpy as jnp
from jax import lax
from jax.experimental import pallas as pl
from jax.experimental.pallas import tpu as pltpu
from jax.sharding import PartitionSpec as P

MESH = pl.DeviceIdType.MESH
OFFSETS = (1, -1, 2, -2, 3, -3)
NI = 1024
CAP = 224
SLOT = 256
SIDES = 6
NC = 24
ROWS = SIDES * SLOT
CHUNKS = 4
WIDE = NI // CHUNKS
N_SUB = 32
N_Z = 8
N_X = 4
N_GRP = 8
REL_BLOCKS = (0, 1, 4, 7)
NCG = 1024
LIMIT = 58 * 1024 * 1024
EARLY = 2
PER = WIDE // 128
TALL = 176
F32 = jnp.float32
BF16 = jnp.bfloat16


def dot(a, b):
    return jnp.dot(a, b, preferred_element_type=F32)


def dot_nt(a, b):
    return lax.dot_general(a, b, (((1,), (1,)), ((), ())), preferred_element_type=F32)


def dot_tn(a, b):
    return lax.dot_general(a, b, (((0,), (0,)), ((), ())), preferred_element_type=F32)


def split(x):
    high = x.astype(BF16)
    return high, (x - high.astype(F32)).astype(BF16)


def kernel(
    u_hbm, f_hbm, s_hbm, k_hbm, p_ref, cinv_hbm, own_ref, idx_ref, cnt_ref,
    new_ref, res_ref,
    u, f, s, k, cinv, slots, pick, pick_t, wcol, wp,
    rb, cb, out1, in1, out2, in2,
    owners, btr, bt, y_out, y_in, terms, terms_in, etr, pieces,
    v_out, v_in, rel_val, own_val, near_val, early,
    load_sem, a1_send, a1_recv, a2_send, a2_recv, y_send, y_recv,
    s1_send, s1_recv, s3_send, s3_recv, s4_send, s4_recv,
    s5_send, s5_recv, s6_send, s6_recv,
):
    g = lax.axis_index("grp")
    a = lax.axis_index("sub")
    z = a // N_X
    x = lax.rem(a, N_X)

    def near(j):
        return {"sub": lax.rem(a + OFFSETS[j] + N_SUB, N_SUB)}

    def along_z(d):
        return {"sub": lax.rem(z + d, N_Z) * N_X + x}

    def along_x(d):
        return {"sub": z * N_X + lax.rem(x + d, N_X)}

    def along_g(d):
        return {"grp": lax.rem(g + d, N_GRP)}

    def remote(src, dst, send, recv, where):
        return pltpu.make_async_remote_copy(
            src_ref=src, dst_ref=dst, send_sem=send, recv_sem=recv,
            device_id=where, device_id_type=MESH,
        )

    loads = [pltpu.make_async_copy(s_hbm, s, load_sem.at[0])]
    for c in range(CHUNKS):
        cols = pl.ds(c * WIDE, WIDE)
        for n, (src, dst) in enumerate(((u_hbm, u), (f_hbm, f))):
            loads.append(
                pltpu.make_async_copy(src.at[:, cols], dst.at[c], load_sem.at[1 + 2 * c + n])
            )
    late_loads = [
        pltpu.make_async_copy(k_hbm, k, load_sem.at[1 + 2 * CHUNKS]),
        pltpu.make_async_copy(cinv_hbm, cinv, load_sem.at[2 + 2 * CHUNKS]),
    ]
    for load in loads + late_loads:
        load.start()

    barrier = pltpu.get_barrier_semaphore()
    partners = [near(j) for j in range(SIDES)]
    partners += [along_z(d) for d in range(1, N_Z)]
    partners += [along_x(d) for d in range(1, N_X)]
    partners += [along_g(d) for d in range(1, N_GRP)]
    for who in partners:
        pl.semaphore_signal(barrier, inc=1, device_id=who, device_id_type=MESH)

    slots[...] = jnp.full((8, SLOT), -1.0, F32)
    slot_ids = lax.broadcasted_iota(jnp.int32, (1, CAP), 1)
    for j in range(SIDES):
        slots[j : j + 1, 0:CAP] = jnp.where(
            slot_ids < cnt_ref[0, j], idx_ref[j].astype(F32), -1.0
        )
    lane = lax.broadcasted_iota(jnp.int32, (SLOT, 128), 1).astype(F32)
    counts = [jnp.zeros((8, 128), F32)] * (NI // 128)
    for j in range(SIDES):
        column = jnp.transpose(jnp.broadcast_to(slots[j : j + 1, :], (128, SLOT)))
        for q in range(NI // 128):
            hot = jnp.where(column == lane + float(128 * q), 1.0, 0.0)
            pick[SLOT * j : SLOT * (j + 1), 128 * q : 128 * (q + 1)] = hot.astype(BF16)
            counts[q] += jnp.sum(hot.reshape(SLOT // 8, 8, 128), axis=0)
    wrow = 1.0 / (1.0 + jnp.sum(jnp.concatenate(counts, axis=1), axis=0, keepdims=True))

    def first(c):
        if c == 0:
            loads[0].wait()
        loads[1 + 2 * c].wait()
        loads[2 + 2 * c].wait()
        rest = (f[c].astype(F32) - dot(s[...], u[c])).astype(BF16)
        rb[c] = rest
        if c > 0:
            out1[c] = dot(pick[...], rest).astype(BF16)

    def assembly_copy(out, into, send, recv, c, j):
        return remote(
            out.at[c, pl.ds(SLOT * j, CAP), :],
            into.at[c, pl.ds(SLOT * (j ^ 1), CAP), :],
            send.at[c, j],
            recv.at[c, j ^ 1],
            near(j),
        )

    def assembly_wait(out, into, send, recv, c, j):
        remote(
            out.at[c, pl.ds(SLOT * j, CAP), :],
            into.at[c, pl.ds(SLOT * j, CAP), :],
            send.at[c, j],
            recv.at[c, j],
            near(j),
        ).wait_recv()

    def send_first(c, sides=range(SIDES)):
        for j in sides:
            assembly_copy(out1, in1, a1_send, a1_recv, c, j).start()

    def send_second(c, sides=range(SIDES)):
        for j in sides:
            assembly_copy(out2, in2, a2_send, a2_recv, c, j).start()

    weighted = p_ref[...].astype(F32) * wrow
    wp[...] = jnp.concatenate([weighted, jnp.zeros((8, NI), F32)], axis=0).astype(BF16)
    owners[...] = jnp.zeros((16, 128), F32)
    owners[8:9, 0:NC] = (own_ref[...] >> 5).astype(F32)
    owners[9:10, 0:NC] = (own_ref[...] & 31).astype(F32)
    low_names = pltpu.roll(jnp.broadcast_to(owners[9:10, :], (8, 128)), 64, 1)
    mine = jnp.broadcast_to(owners[8:9, :], (8, 128)) + low_names
    for j in range(SIDES):
        rows = dot_nt(wp[...], pick[SLOT * j : SLOT * (j + 1), :])
        tail = jnp.concatenate([mine, jnp.zeros((8, SLOT - 128), F32)], axis=1)
        y_out[j] = jnp.concatenate([rows[0:NC], tail], axis=0).astype(BF16)
    first(0)
    pl.semaphore_wait(barrier, len(partners))
    for j in range(SIDES):
        remote(y_out.at[j], y_in.at[j ^ 1], y_send.at[j], y_recv.at[j ^ 1], near(j)).start()
    for j in range(SIDES):
        rows = slice(SLOT * j, SLOT * (j + 1))
        out1[0, rows, :] = dot(pick[rows, :], rb[0]).astype(BF16)
        send_first(0, (j,))


    for c in range(1, CHUNKS):
        first(c)
        if c < 2:
            send_first(c)

    for j in range(SIDES):
        remote(y_out.at[j], y_in.at[j], y_send.at[j], y_recv.at[j], near(j)).wait_recv()
    blocks = []
    for t in range(7):
        if t == 3:
            blocks.append(wp[0:NC, :].astype(F32))
            owners[t : t + 1, :] = mine[0:1, :]
        else:
            j = OFFSETS.index(t - 3)
            blocks.append(dot(y_in[j], pick[SLOT * j : SLOT * (j + 1), :])[0:NC])
            owners[t : t + 1, :] = y_in[j, NC:32, 0:128].astype(F32)[0:1, :]
    blocks.append(jnp.zeros((256 - 7 * NC, NI), F32))
    every = jnp.concatenate(blocks, axis=0)
    btr[...] = every[0:TALL].astype(BF16)
    for c in range(CHUNKS):
        part = dot(btr[...], rb[c])
        for q in range(PER):
            terms[c * PER + q] = jnp.concatenate(
                [part[0 : 7 * NC, 128 * q : 128 * (q + 1)], owners[0:8, :]], axis=0
            ).astype(BF16)

    def z_copy(d):
        there = lax.rem(z + d, N_Z)
        return remote(
            terms.at[there], terms_in.at[z], s1_send.at[d - 1], s1_recv.at[d - 1], along_z(d)
        )

    for d in range(1, N_Z):
        z_copy(d).start()
    send_first(2)
    terms_in[z] = terms[z]

    up = lax.broadcasted_iota(jnp.int32, (NI, SLOT), 0).astype(F32)
    for j in range(SIDES):
        pick_t[:, SLOT * j : SLOT * (j + 1)] = jnp.where(
            slots[j : j + 1, :] == up, 1.0, 0.0
        ).astype(BF16)
    wcol[...] = 1.0 / (1.0 + dot(pick_t[...], jnp.ones((ROWS, 128), BF16)))
    for c in range(CHUNKS):
        for j in range(SIDES):
            rows = slice(SLOT * j + CAP, SLOT * (j + 1))
            in1[c, rows, :] = jnp.zeros((SLOT - CAP, WIDE), BF16)
            in2[c, rows, :] = jnp.zeros((SLOT - CAP, WIDE), BF16)
    for n in range(N_Z):
        near_val[n, TALL:256, :] = jnp.zeros((256 - TALL, 128), BF16)
    for load in late_loads:
        load.wait()

    bt[...] = jnp.transpose(every).astype(BF16)
    for d in range(1, N_Z):
        here = lax.rem(z + N_Z - d, N_Z)
        remote(
            terms.at[z], terms_in.at[here], s1_send.at[d - 1], s1_recv.at[d - 1], along_z(d)
        ).wait_recv()

    weights = jnp.concatenate([wcol[...]] * (WIDE // 128), axis=1)

    def second(c):
        for j in range(SIDES):
            assembly_wait(out1, in1, a1_send, a1_recv, c, j)
        total = rb[c].astype(F32) + dot(pick_t[...], in1[c])
        res_ref[:, c * WIDE : (c + 1) * WIDE] = total.astype(BF16)
        scaled = (weights * total).astype(BF16)
        local = (weights * dot(k[...], scaled)).astype(BF16)
        cb[c] = local
        out2[c] = dot(pick[...], local).astype(BF16)

    column512 = lax.broadcasted_iota(jnp.int32, (NC, 512), 1)
    block = column512 // 128
    start = block + 2 * (block // 2) + 2 * (block // 3)
    names = (column512 + 128 * (start - block)).astype(F32)
    base = (g * 128).astype(F32)
    turned = jnp.transpose(
        jnp.concatenate([terms_in[n, TALL - 16 : TALL, :].astype(F32)[8:16] for n in range(N_Z)], axis=0)
    )
    who = turned[0:NC, :] * 32.0 + turned[64 : 64 + NC, :]
    rel = who - base
    rel = jnp.where(rel < 0.0, rel + float(NCG), rel)
    for n in range(N_Z):
        hot = [
            jnp.where(rel[:, 8 * n + t : 8 * n + t + 1] == names, 1.0, 0.0) for t in range(7)
        ]
        hot.append(jnp.zeros((8, 512), F32))
        etr[TALL * n : TALL * (n + 1), :] = jnp.concatenate(hot, axis=0).astype(BF16)
    sums = dot_tn(etr[...], terms_in[...].reshape(N_Z * TALL, 128))
    pieces[g] = sums.astype(BF16).reshape(4, 128, 128)

    def g_copy(d):
        return remote(
            pieces.at[g], pieces.at[g], s3_send.at[d - 1], s3_recv.at[d - 1], along_g(d)
        )

    for d in range(1, N_GRP):
        g_copy(d).start()
    send_first(3)
    second(0)
    send_second(0, range(3))
    second(1)
    send_second(0, range(3, SIDES))
    for d in range(1, N_GRP):
        here = lax.rem(g + N_GRP - d, N_GRP)
        remote(
            pieces.at[g], pieces.at[here], s3_send.at[d - 1], s3_recv.at[d - 1], along_g(d)
        ).wait_recv()
    whole = [
        sum(pieces[(n - r) % N_GRP, q].astype(F32) for q, r in enumerate(REL_BLOCKS))
        for n in range(N_GRP)
    ]
    high, low = split(jnp.concatenate(whole, axis=0))
    chigh, clow = split(cinv[...])
    partial = dot(chigh, high) + (dot(clow, high) + dot(chigh, low))
    v_out[0] = partial.astype(BF16)

    def v_copy(d):
        return remote(
            v_out.at[0], v_in.at[d - 1], s4_send.at[d - 1], s4_recv.at[d - 1], along_x(d)
        )

    for d in range(1, N_X):
        v_copy(d).start()
    second(2)
    send_second(1)
    second(3)
    send_second(2)
    for d in range(1, N_X):
        v_copy(d).wait_recv()
    solved = v_out[0].astype(F32)
    for d in range(1, N_X):
        solved += v_in[d - 1].astype(F32)
    rel_val[0] = solved.astype(BF16)

    def r_copy(n):
        return remote(
            rel_val.at[0], rel_val.at[n], s5_send.at[n - 1], s5_recv.at[n - 1],
            along_g((7, 4, 1)[n - 1]),
        )

    for n in range(1, 4):
        r_copy(n).start()
    send_second(3, range(3))
    for n in range(1, 4):
        r_copy(n).wait_recv()
    own_val[...] = dot(etr[...], rel_val[...].reshape(512, 128)).astype(BF16).reshape(N_Z, TALL, 128)

    def o_copy(d):
        there = lax.rem(z + d, N_Z)
        return remote(
            own_val.at[there], near_val.at[z, pl.ds(0, TALL)],
            s6_send.at[d - 1], s6_recv.at[d - 1], along_z(d),
        )

    for d in range(1, N_Z):
        o_copy(d).start()
    send_second(3, range(3, SIDES))
    near_val[z, pl.ds(0, TALL)] = own_val[z]

    def second_sum(c):
        for j in range(SIDES):
            assembly_wait(out2, in2, a2_send, a2_recv, c, j)
        return u[c].astype(F32) + (cb[c].astype(F32) + dot(pick_t[...], in2[c]))

    for c in range(EARLY):
        early[c] = second_sum(c)
    for d in range(1, N_Z):
        here = lax.rem(z + N_Z - d, N_Z)
        remote(
            own_val.at[z], near_val.at[here, pl.ds(0, TALL)],
            s6_send.at[d - 1], s6_recv.at[d - 1], along_z(d),
        ).wait_recv()

    def third(c):
        coarse = dot(bt[...], jnp.concatenate([near_val[c * PER + q] for q in range(PER)], axis=1))
        if c < EARLY:
            total = early[c] + coarse
        else:
            total = u[c].astype(F32) + (cb[c].astype(F32) + coarse)
            step = 2 if c == CHUNKS - 1 else SIDES
            for low in range(0, SIDES, step):
                for j in range(low, low + step):
                    assembly_wait(out2, in2, a2_send, a2_recv, c, j)
                rows = slice(SLOT * low, SLOT * (low + step))
                total += dot(pick_t[:, rows], in2[c, rows, :])
        new_ref[:, c * WIDE : (c + 1) * WIDE] = total.astype(BF16)

    for c in range(CHUNKS):
        third(c)

    for c in range(CHUNKS):
        for j in range(SIDES):
            assembly_copy(out1, in1, a1_send, a1_recv, c, j).wait_send()
            assembly_copy(out2, in2, a2_send, a2_recv, c, j).wait_send()
    for j in range(SIDES):
        remote(y_out.at[j], y_in.at[j ^ 1], y_send.at[j], y_recv.at[j ^ 1], near(j)).wait_send()
    for d in range(1, N_Z):
        z_copy(d).wait_send()
        o_copy(d).wait_send()
        g_copy(d).wait_send()
    for d in range(1, N_X):
        v_copy(d).wait_send()
    for n in range(1, 4):
        r_copy(n).wait_send()


def on_device(
    iterate, load, schur, local_inverse, basis, coarse_inverse, owner, shared_index, shared_count
):
    anywhere = pl.BlockSpec(memory_space=pltpu.HBM)
    vmem = pl.BlockSpec(memory_space=pltpu.VMEM)
    smem = pl.BlockSpec(memory_space=pltpu.SMEM)
    dma = pltpu.SemaphoreType.DMA

    def bf16(*shape):
        return pltpu.VMEM(shape, BF16)

    def f32(*shape):
        return pltpu.VMEM(shape, F32)

    chunk = (CHUNKS, NI, WIDE)
    side = (CHUNKS, ROWS, WIDE)
    new, residual = pl.pallas_call(
        kernel,
        out_shape=(bf16(NI, NI), bf16(NI, NI)),
        in_specs=[anywhere, anywhere, anywhere, anywhere, vmem, anywhere, vmem, vmem, smem],
        out_specs=(vmem, vmem),
        scratch_shapes=[
            bf16(*chunk), bf16(*chunk), bf16(NI, NI), bf16(NI, NI), f32(128, NI),
            f32(8, SLOT), bf16(ROWS, NI), bf16(NI, ROWS), f32(NI, 128), bf16(32, NI),
            bf16(*chunk), bf16(*chunk), bf16(*side), bf16(*side), bf16(*side), bf16(*side),
            f32(16, 128), bf16(TALL, NI), bf16(NI, 256),
            bf16(SIDES, 32, SLOT), bf16(SIDES, 32, SLOT),
            bf16(N_Z, TALL, 128), bf16(N_Z, TALL, 128), bf16(N_Z * TALL, 512),
            bf16(N_GRP, 4, 128, 128),
            bf16(1, 128, 128), bf16(3, 128, 128), bf16(4, 128, 128),
            bf16(N_Z, TALL, 128), bf16(N_Z, 256, 128), f32(EARLY, NI, WIDE),
            dma((3 + 2 * CHUNKS,)),
            dma((CHUNKS, SIDES)), dma((CHUNKS, SIDES)), dma((CHUNKS, SIDES)), dma((CHUNKS, SIDES)),
            dma((SIDES,)), dma((SIDES,)),
            dma((7,)), dma((7,)), dma((7,)), dma((7,)),
            dma((3,)), dma((3,)), dma((3,)), dma((3,)), dma((7,)), dma((7,)),
        ],
        compiler_params=pltpu.CompilerParams(
            collective_id=0, has_side_effects=True, vmem_limit_bytes=LIMIT
        ),
        name="bddc_step",
    )(
        iterate, load, schur, local_inverse, basis, coarse_inverse, owner,
        jnp.transpose(shared_index, (1, 0, 2)), shared_count,
    )
    return new, residual


def solution(mesh):
    rows = P(("grp", "sub"), None)
    placed = (rows, rows, rows, rows, rows, P("grp", None), rows, P(("grp", "sub"), None, None), rows)
    return jax.shard_map(
        on_device, mesh=mesh, in_specs=placed, out_specs=(rows, rows), check_vma=False
    )
```
